256 devices in a mesh: tile: 32 (over y, z), freq: 8 (over x, core).
Axes of the slice: x: 4, y: 4, z: 8, core: 2. Of those that a mesh axis runs over, the one named last changes fastest.
Arguments:
- visibilities: float32 [8, 4096, 2, 128], P('freq', 'tile'), may hold values from -6 to 6
- uv_cell: int32 [8, 4096, 2, 128], P('freq', 'tile'), may hold values from 0 to 120
- sub_pixel: int32 [8, 4096, 2, 128], P('freq', 'tile'), may hold values from 0 to 7
- w_plane: int32 [8, 4096], P('freq', 'tile'), may hold values from 0 to 15
- block_tile: int32 [8, 4096], P('freq', 'tile'), may hold values from 0 to 63, as said below
- model_grid: bfloat16 [8, 64, 128, 256], P('freq', 'tile'), may hold values from -3 to 3
- kernel_table: bfloat16 [16, 8, 8], replicated, may hold values from 0.049804688 to 1
- coupling: float32 [8, 8], replicated, may hold values from -2 to 2
Outputs:
- residuals: float32 [8, 4096, 2, 128], P('freq', 'tile')
- coupled_grid: float32 [8, 64, 128, 256], P('freq', 'tile')
The draws below stay inside these ranges and needn't reach their ends.
Inputs may be any that keep to these rules, and one draw needn't show every extreme that they name: `block_tile`: among the 128 blocks of one plane on one device (aligned blocks), at most 12 have tiles of one owner, the owner of tile k being k // 2; in every plane some owner gets exactly 12 blocks from every device.
All inputs are finite; a program needn't handle non-finite values.
Results may differ from the reference program's by a relative error of at most 0.0034.
Values may be sent and summed in bfloat16 or wider, within the bound.
A program may use at most 64 MiB of HBM per device.

```python
import math
import jax
import jax.numpy as jnp
from jax import lax

TS = 128
KS = 8
OS = 8
W_PLANES = 16
ROWS = 128
TILES_DEV = 2
BLK_DEV = 128
FREQ = 8
TILES = 64
BLOCKS = 4096
CAP = 12


def draw_block_tile(key, part):
    owners = BLOCKS // BLK_DEV
    position_holders = owners * CAP
    hottest = jax.random.randint(jax.random.fold_in(key, 11), (FREQ,), 0, owners)
    device_base = jax.random.fold_in(key, 23)

    def one_device(index):
        plane = index // owners
        device_key = jax.random.fold_in(device_base, index)
        noise_key, tile_key, order_key = jax.random.split(device_key, 3)
        slot_owner = jnp.arange(position_holders, dtype=jnp.int32) // CAP
        ahead = (slot_owner - hottest[plane]) % owners
        separation_gap = jnp.minimum(ahead, owners - ahead)
        reward_extra = jnp.where(separation_gap == 0, 8, jnp.maximum(0, 3 - separation_gap))
        random_jitter = jax.random.randint(noise_key, (position_holders,), 0, 4096)
        rating_value = (reward_extra * 4096 + random_jitter) * position_holders + jnp.arange(position_holders, dtype=jnp.int32)
        chosen = lax.top_k(rating_value, BLK_DEV)[1]
        owner = chosen // CAP
        local = jax.random.randint(tile_key, (BLK_DEV,), 0, TILES_DEV)
        order = jax.random.permutation(order_key, BLK_DEV)
        return (owner * TILES_DEV + local)[order].astype(jnp.int32)
    tiles = jax.vmap(one_device)(jnp.arange(FREQ * owners, dtype=jnp.int32))
    return tiles.reshape(FREQ, BLOCKS)


def plant(drawn, own_key, smallest, top_value):
    spot = [jax.random.randint(jax.random.fold_in(own_key, axis), (), 0, length) for axis, length in enumerate(drawn.shape)]
    longest = drawn.shape.index(max(drawn.shape))
    beside = spot[:longest] + [(spot[longest] + 1) % drawn.shape[longest]] + spot[longest + 1:]
    return drawn.at[tuple(spot)].set(smallest).at[tuple(beside)].set(top_value)


def block_levels(key, dims, cuts, low, largest):
    level = 1.0
    for position, blocks in cuts:
        heights = jax.random.uniform(jax.random.fold_in(jax.random.fold_in(key, 6), position), (blocks,), jnp.float32, low / len(cuts), largest / len(cuts))
        level = level * jnp.repeat(jnp.exp(heights), dims[position] // blocks).reshape((-1,) + (1,) * (len(dims) - 1 - position))
    return level


def normal_values(key, dims, spread, reach, cuts=(), kind=jnp.bfloat16):
    loudness = block_levels(key, dims, cuts, -0.22, 0.18) if cuts else 1.0
    result = jax.random.normal(key, dims, jnp.float32) * spread * loudness
    return jnp.minimum(jnp.maximum(result, -reach), reach).astype(kind)


def setup_inputs(seed: int = 0) -> dict:
    seeds = jax.random.split(jax.random.key(seed), 9)
    return {
        "visibilities": normal_values(seeds[0], (FREQ, BLOCKS, 2, ROWS), 1.0, 6.0, ((0, 8), (1, 32)), jnp.float32),
        "uv_cell": plant(jax.random.randint(seeds[1], (FREQ, BLOCKS, 2, ROWS), 0, TS - KS + 1), jax.random.fold_in(seeds[1], 1), 0, TS - KS).astype(jnp.int32),
        "sub_pixel": plant(jax.random.randint(seeds[2], (FREQ, BLOCKS, 2, ROWS), 0, OS), jax.random.fold_in(seeds[2], 1), 0, OS - 1).astype(jnp.int32),
        "w_plane": plant(jax.random.randint(seeds[3], (FREQ, BLOCKS), 0, W_PLANES), jax.random.fold_in(seeds[3], 1), 0, W_PLANES - 1).astype(jnp.int32),
        "block_tile": draw_block_tile(jax.random.fold_in(seeds[8], 71), 0),
        "model_grid": normal_values(seeds[5], (FREQ, TILES, TS, 2 * TS), 0.5, 3.0, ((0, 8), (1, 32))),
        "kernel_table": jnp.clip(jnp.exp(jax.random.uniform(seeds[6], (W_PLANES, OS, KS), jnp.float32, math.log(0.049804688), math.log(1.0))), 0.049804688, 1.0).astype(jnp.bfloat16),
        "coupling": normal_values(seeds[7], (FREQ, FREQ), FREQ ** -0.5, 2.0, (), jnp.float32),
    }


def plane_work(samples, cells, offsets, planes, tiles, model, kernel_table):
    cluster_count = 256
    count = samples.shape[0] // cluster_count
    spans = jnp.arange(KS, dtype=jnp.int32)

    def advance(grid_sum, pieces):
        sample_part, cell_part, offset_part, plane_part, tile_part = pieces
        row_taps = kernel_table[plane_part[:, None], offset_part[:, 0, :]].astype(jnp.float32)
        column_taps = kernel_table[plane_part[:, None], offset_part[:, 1, :]].astype(jnp.float32)
        cell_rows = cell_part[:, 0, :, None, None] + spans[None, None, :, None]
        cell_columns = cell_part[:, 1, :, None, None] + spans[None, None, None, :]
        tile_index = tile_part[:, None, None, None]
        real_patch = model[tile_index, cell_rows, cell_columns].astype(jnp.float32)
        imag_patch = model[tile_index, cell_rows, cell_columns + TS].astype(jnp.float32)
        outer = row_taps[:, :, :, None] * column_taps[:, :, None, :]
        model_real = jnp.sum(real_patch * outer, axis=(2, 3))
        model_imag = jnp.sum(imag_patch * outer, axis=(2, 3))
        residual = sample_part - jnp.stack([model_real, model_imag], axis=1)
        weighted = (residual[:, :, :, None] * column_taps[:, None, :, :]).astype(jnp.bfloat16)
        weighted = lax.optimization_barrier(weighted).astype(jnp.float32)
        add_real = row_taps[:, :, :, None] * weighted[:, 0, :, None, :]
        imaginary_addend = row_taps[:, :, :, None] * weighted[:, 1, :, None, :]
        grid_sum = grid_sum.at[tile_index, cell_rows, cell_columns].add(add_real)
        grid_sum = grid_sum.at[tile_index, cell_rows, cell_columns + TS].add(imaginary_addend)
        return grid_sum, residual

    def split(values):
        return values.reshape((count, cluster_count) + values.shape[1:])

    start_grid = jnp.zeros((TILES, TS, 2 * TS), jnp.float32)
    grid_sum, residual = lax.scan(advance, start_grid, (split(samples), split(cells), split(offsets), split(planes), split(tiles)))
    return grid_sum, residual.reshape(samples.shape)


def reference(visibilities, uv_cell, sub_pixel, w_plane, block_tile, model_grid, kernel_table, coupling):
    def one_plane(pieces):
        return plane_work(pieces[0], pieces[1], pieces[2], pieces[3], pieces[4], pieces[5], kernel_table)

    grids, residuals = lax.map(one_plane, (visibilities, uv_cell, sub_pixel, w_plane, block_tile, model_grid))
    rounded = grids.astype(jnp.bfloat16).astype(jnp.float32)
    coupled_grid = jnp.einsum("fg,gtij->ftij", coupling, rounded, precision=lax.Precision.HIGHEST)
    return residuals, coupled_grid
```

```python
import functools

import jax
import jax.numpy as jnp
from jax import lax
from jax.experimental import pallas as pl
from jax.experimental.pallas import tpu as pltpu
from jax.sharding import PartitionSpec as P

SHIFT = 65536


def spread(start, table_row, table, lanes):
    sub = lax.broadcasted_iota(jnp.int32, (8, lanes), 0)
    taps = jnp.take_along_axis(table, jnp.broadcast_to(table_row, (8, lanes)), axis=1, mode="promise_in_bounds")
    offset = sub - start
    folded = jnp.take_along_axis(taps, jnp.bitwise_and(offset, 7), axis=0, mode="promise_in_bounds")
    return folded, lax.shift_right_arithmetic(offset, 3)


def twice(folded, group):
    values = jnp.concatenate([folded, folded], axis=0).astype(jnp.bfloat16)
    groups = jnp.concatenate([group, group + 1], axis=0).astype(jnp.float32).astype(jnp.bfloat16)
    return values, groups


def work_chunk(rec, model_t, table, row_ref, weighted_ref, emit, capacity, side):
    lanes = 128
    zero16 = jnp.zeros((16, lanes), jnp.bfloat16)
    column = []
    for k in range(capacity):
        position = rec(k, 2).astype(jnp.int32)
        lookup = rec(k, 3).astype(jnp.int32)
        folded, group = spread(lax.shift_right_logical(position, 16), lax.shift_right_logical(lookup, 16), table, lanes)
        values, groups = twice(folded, group)
        for tile in range(2 * side // 16):
            row_ref[pl.ds(16 * tile, 16), pl.ds(k * lanes, lanes)] = jnp.where(
                groups == jnp.bfloat16(-2 * tile), values, zero16
            )
        column.append(
            spread(jnp.bitwise_and(position, SHIFT - 1), jnp.bitwise_and(lookup, SHIFT - 1), table, lanes)
        )
    for pair in range(capacity // 2):
        partial = jnp.dot(
            model_t, row_ref[:, pl.ds(pair * 2 * lanes, 2 * lanes)], preferred_element_type=jnp.float32
        )
        for half in range(2):
            k = 2 * pair + half
            folded, group = column[k]
            block = partial[:, half * lanes : (half + 1) * lanes]
            picked = [jnp.zeros((8, lanes), jnp.float32)] * 2
            for tile in range(side // 8):
                hit = group == -tile
                for part in range(2):
                    start = part * side + 8 * tile
                    picked[part] = jnp.where(hit, block[start : start + 8], picked[part])
            for part in range(2):
                residual = rec(k, part) - jnp.sum(picked[part] * folded, axis=0, keepdims=True)
                emit(k, part, residual)
                values, groups = twice(residual * folded, group)
                for tile in range(side // 16):
                    weighted_ref[pl.ds(part * side + 16 * tile, 16), pl.ds(k * lanes, lanes)] = jnp.where(
                        groups == jnp.bfloat16(-2 * tile), values, zero16
                    )


def compute_kernel(capacity, side, rec_ref, model_ref, table_ref, residual_ref, grid_ref, row_ref, weighted_ref, total_ref):
    step = pl.program_id(0)

    @pl.when(step == 0)
    def _():
        total_ref[...] = jnp.zeros_like(total_ref)

    def rec(k, which):
        return rec_ref[0, k, pl.ds(which, 1), :]

    def emit(k, part, value):
        residual_ref[0, k, pl.ds(part, 1), :] = value

    work_chunk(rec, model_ref[...], table_ref[...], row_ref, weighted_ref, emit, capacity, side)
    total_ref[...] += lax.dot_general(
        row_ref[...], weighted_ref[...], (((1,), (1,)), ((), ())), preferred_element_type=jnp.float32
    )

    @pl.when(step == pl.num_programs(0) - 1)
    def _():
        grid_ref[...] = total_ref[...].astype(jnp.bfloat16)


def degrid_grid(records, model, table):
    owners, capacity = records.shape[:2]
    tiles, side = model.shape[0], model.shape[1]
    model_t = model.reshape(tiles * side, 2 * side).T
    return pl.pallas_call(
        functools.partial(compute_kernel, capacity, side),
        grid=(owners,),
        out_shape=(
            jax.ShapeDtypeStruct((owners, capacity, 2, 128), jnp.float32),
            jax.ShapeDtypeStruct((tiles * side, 2 * side), jnp.bfloat16),
        ),
        in_specs=[
            pl.BlockSpec((1, capacity, 4, 128), lambda i: (i, 0, 0, 0)),
            pl.BlockSpec((2 * side, tiles * side), lambda i: (0, 0)),
            pl.BlockSpec((8, 128), lambda i: (0, 0)),
        ],
        out_specs=[
            pl.BlockSpec((1, capacity, 2, 128), lambda i: (i, 0, 0, 0)),
            pl.BlockSpec((tiles * side, 2 * side), lambda i: (0, 0)),
        ],
        scratch_shapes=[
            pltpu.VMEM((tiles * side, capacity * 128), jnp.bfloat16),
            pltpu.VMEM((2 * side, capacity * 128), jnp.bfloat16),
            pltpu.VMEM((tiles * side, 2 * side), jnp.float32),
        ],
        compiler_params=pltpu.CompilerParams(vmem_limit_bytes=32 << 20),
    )(records, model_t, table)


def body(visibilities, uv_cell, sub_pixel, w_plane, block_tile, model_grid, kernel_table, coupling):
    blocks = visibilities.shape[1]
    rows = visibilities.shape[3]
    owners = lax.axis_size("tile")
    capacity = 3 * blocks // owners
    total = owners * capacity
    tiles_here = model_grid.shape[1]
    side = model_grid.shape[2]
    oversample = kernel_table.shape[1]
    support = kernel_table.shape[2]
    tile_id = block_tile[0]
    owner = tile_id // tiles_here
    local_tile = tile_id % tiles_here
    order = jnp.arange(blocks, dtype=jnp.int32)
    same = (owner[:, None] == owner[None, :]) & (order[None, :] < order[:, None])
    slot = owner * capacity + jnp.sum(same.astype(jnp.int32), axis=1)
    holds = slot[None, :] == jnp.arange(total, dtype=jnp.int32)[:, None]
    source = jnp.sum(jnp.where(holds, order[None, :], 0), axis=1)
    filled = jnp.any(holds, axis=1)
    cells = uv_cell[0]
    lookup = w_plane[0][:, None, None] * oversample + sub_pixel[0]
    position = (cells[:, 0] + side * local_tile[:, None]) * SHIFT + cells[:, 1]
    records = jnp.concatenate(
        [
            visibilities[0],
            position[:, None].astype(jnp.float32),
            (lookup[:, 0] * SHIFT + lookup[:, 1])[:, None].astype(jnp.float32),
        ],
        axis=1,
    )
    empty = jnp.array([0.0, 0.0, tiles_here * side * SHIFT, 0.0], jnp.float32)[None, :, None]
    sent = jnp.where(filled[:, None, None], jnp.take(records, source, axis=0), empty)
    got = lax.all_to_all(sent.reshape(owners, capacity, 4, rows), "tile", split_axis=0, concat_axis=0, tiled=True)
    table = kernel_table.reshape(-1, support).T.astype(jnp.float32)
    residual, grid_rounded = degrid_grid(got, model_grid[0], table)
    returned = lax.all_to_all(residual, "tile", split_axis=0, concat_axis=0, tiled=True)
    residuals = jnp.take(returned.reshape(total, 2, rows), slot, axis=0)[None]
    grid_rounded = grid_rounded.reshape(1, tiles_here, side, 2 * side)
    own_row = lax.dynamic_index_in_dim(coupling, lax.axis_index("freq"), 0, keepdims=False)
    coupled_grid = jnp.sum(
        own_row[:, None, None, None]
        * lax.all_gather(grid_rounded, "freq", axis=0, tiled=True).astype(jnp.float32),
        axis=0,
    )[None]
    return (residuals, coupled_grid)


def solution(mesh):
    return jax.shard_map(
        body,
        mesh=mesh,
        in_specs=(
            P("freq", "tile", None, None),
            P("freq", "tile", None, None),
            P("freq", "tile", None, None),
            P("freq", "tile"),
            P("freq", "tile"),
            P("freq", "tile", None, None),
            P(),
            P(),
        ),
        out_specs=(P("freq", "tile", None, None), P("freq", "tile", None, None)),
        check_vma=False,
    )
```

```python
import functools

import jax
import jax.numpy as jnp
from jax import lax
from jax.experimental import pallas as pl
from jax.experimental.pallas import tpu as pltpu
from jax.sharding import PartitionSpec as P

SHIFT = 65536


def spread(start, table_row, table, lanes):
    sub = lax.broadcasted_iota(jnp.int32, (8, lanes), 0)
    taps = jnp.take_along_axis(table, jnp.broadcast_to(table_row, (8, lanes)), axis=1, mode="promise_in_bounds")
    offset = sub - start
    folded = jnp.take_along_axis(taps, jnp.bitwise_and(offset, 7), axis=0, mode="promise_in_bounds")
    return folded, lax.shift_right_arithmetic(offset, 3)


def twice(folded, group):
    values = jnp.concatenate([folded, folded], axis=0).astype(jnp.bfloat16)
    groups = jnp.concatenate([group, group + 1], axis=0).astype(jnp.float32).astype(jnp.bfloat16)
    return values, groups


def work_chunk(rec, model_t, table, row_ref, weighted_ref, emit, capacity, side):
    lanes = 128
    zero16 = jnp.zeros((16, lanes), jnp.bfloat16)
    column = []
    for k in range(capacity):
        position = rec(k, 2).astype(jnp.int32)
        lookup = rec(k, 3).astype(jnp.int32)
        folded, group = spread(lax.shift_right_logical(position, 16), lax.shift_right_logical(lookup, 16), table, lanes)
        values, groups = twice(folded, group)
        for tile in range(2 * side // 16):
            row_ref[pl.ds(16 * tile, 16), pl.ds(k * lanes, lanes)] = jnp.where(
                groups == jnp.bfloat16(-2 * tile), values, zero16
            )
        column.append(
            spread(jnp.bitwise_and(position, SHIFT - 1), jnp.bitwise_and(lookup, SHIFT - 1), table, lanes)
        )
    for pair in range(capacity // 2):
        partial = jnp.dot(
            model_t, row_ref[:, pl.ds(pair * 2 * lanes, 2 * lanes)], preferred_element_type=jnp.float32
        )
        for half in range(2):
            k = 2 * pair + half
            folded, group = column[k]
            block = partial[:, half * lanes : (half + 1) * lanes]
            picked = [jnp.zeros((8, lanes), jnp.float32)] * 2
            for tile in range(side // 8):
                hit = group == -tile
                for part in range(2):
                    start = part * side + 8 * tile
                    picked[part] = jnp.where(hit, block[start : start + 8], picked[part])
            for part in range(2):
                residual = rec(k, part) - jnp.sum(picked[part] * folded, axis=0, keepdims=True)
                emit(k, part, residual)
                values, groups = twice(residual * folded, group)
                for tile in range(side // 16):
                    weighted_ref[pl.ds(part * side + 16 * tile, 16), pl.ds(k * lanes, lanes)] = jnp.where(
                        groups == jnp.bfloat16(-2 * tile), values, zero16
                    )


MESH = pl.DeviceIdType.MESH


def kernel(
    dims,
    tile_s, plane_s, coupling_s, tile_v, samples, cells, offsets, model, table_ref,
    residual_out, coupled_out,
    records, index_v, index_s, model_t, send, got, solved, returned,
    row0, row1, weighted0, weighted1, total, grids,
    index_sem, send_sem, got_sem, back_sem, home_sem, grid_send, grid_got,
):
    owners, capacity, tiles, side, oversample, chips_y, chips_x = dims
    chips_z = owners // chips_y
    blocks = samples.shape[0]
    lanes = 128
    me = lax.axis_index("tile")
    plane = lax.axis_index("freq")
    mine_y, mine_z = me // chips_z, lax.rem(me, chips_z)
    mine_x, core = plane // 2, lax.rem(plane, 2)

    def hop(n):
        group, across = n // chips_y, lax.rem(n, chips_y)
        along = (group + 1) // 2 * (2 * lax.rem(group, 2) - 1)
        return across, along

    def target(n):
        across, along = hop(n)
        return lax.rem(mine_y + across, chips_y) * chips_z + lax.rem(mine_z + along + chips_z, chips_z)

    def origin(n):
        across, along = hop(n)
        return lax.rem(mine_y - across + chips_y, chips_y) * chips_z + lax.rem(mine_z - along + chips_z, chips_z)

    sibling = 2 * mine_x + 1 - core
    ahead = 2 * lax.rem(mine_x + 1, chips_x) + core
    behind = 2 * lax.rem(mine_x + chips_x - 1, chips_x) + core
    opposite = 2 * lax.rem(mine_x + 2, chips_x) + core

    barrier = pltpu.get_barrier_semaphore()

    def greet(n, carry):
        pl.semaphore_signal(barrier, inc=1, device_id=(target(n), plane), device_id_type=MESH)
        return carry

    lax.fori_loop(1, owners, greet, 0)
    for other in (sibling, ahead, behind):
        pl.semaphore_signal(barrier, inc=1, device_id=(me, other), device_id_type=MESH)

    owner = lax.shift_right_logical(tile_v[...], tiles.bit_length() - 1)
    wide = (blocks, lanes)
    down = lax.broadcasted_iota(jnp.int32, wide, 0)
    over = lax.broadcasted_iota(jnp.int32, wide, 1)

    def stand(row):
        return jnp.broadcast_to(row.astype(jnp.float32), wide).T.astype(jnp.int32)

    same = (stand(owner) == owner) & (down < over)
    slot = owner * capacity + jnp.sum(same.astype(jnp.int32), axis=0, keepdims=True)
    slots = stand(slot)
    for part in range(owners * capacity // lanes):
        index_v[pl.ds(part, 1), :] = blocks + jnp.sum(
            jnp.where(slots == over + part * lanes, down - blocks, 0), axis=0, keepdims=True
        )
    index_v[pl.ds(owners * capacity // lanes, 1), :] = slot
    index_copy = pltpu.make_async_copy(index_v, index_s, index_sem)
    index_copy.start()

    def fill(b, carry):
        tile = lax.rem(tile_s[0, b], tiles)
        base = plane_s[0, b] * oversample
        records[b, pl.ds(0, 2), :] = samples[b]
        place = (cells[b, pl.ds(0, 1), :] + tile * side) * SHIFT + cells[b, pl.ds(1, 1), :]
        lookup = (offsets[b, pl.ds(0, 1), :] + base) * SHIFT + offsets[b, pl.ds(1, 1), :] + base
        records[b, pl.ds(2, 1), :] = place.astype(jnp.float32)
        records[b, pl.ds(3, 1), :] = lookup.astype(jnp.float32)
        return carry

    lax.fori_loop(0, blocks, fill, 0, unroll=8)
    records[blocks] = jnp.where(
        lax.broadcasted_iota(jnp.int32, (4, lanes), 0) == 2, jnp.float32(tiles * side * SHIFT), jnp.float32(0)
    )
    index_copy.wait()
    pl.semaphore_wait(barrier, owners + 2)

    def outward(n):
        to = target(n)
        return pltpu.make_async_remote_copy(
            src_ref=send.at[to], dst_ref=got.at[me], send_sem=send_sem.at[to], recv_sem=got_sem.at[me],
            device_id=(to, plane), device_id_type=MESH,
        )

    def pack(to):
        for j in range(capacity):
            s = to * capacity + j
            send[to, j] = records[index_s[s // lanes, lax.rem(s, lanes)]]

    def dispatch(n, carry):
        pack(target(n))
        outward(n).start()
        return carry

    lax.fori_loop(1, owners, dispatch, 0)
    pack(me)
    own = pltpu.make_async_copy(send.at[me], got.at[me], got_sem.at[me])
    own.start()
    model_t[...] = model[...].T
    total[...] = jnp.zeros_like(total)
    row1[...] = jnp.zeros_like(row1)
    weighted1[...] = jnp.zeros_like(weighted1)

    def arrival(n):
        source = origin(n)
        return pltpu.make_async_remote_copy(
            src_ref=send.at[source], dst_ref=got.at[source], send_sem=send_sem.at[source],
            recv_sem=got_sem.at[source], device_id=(source, plane), device_id_type=MESH,
        )

    def homeward(n):
        to = origin(n)
        return pltpu.make_async_remote_copy(
            src_ref=solved.at[to], dst_ref=returned.at[pl.ds(me * capacity, capacity)],
            send_sem=back_sem.at[to], recv_sem=home_sem.at[me], device_id=(to, plane), device_id_type=MESH,
        )

    def add_grid(weighted, row):
        total[...] += lax.dot_general(
            weighted[...], row[...], (((1,), (1,)), ((), ())), preferred_element_type=jnp.float32
        )

    def chunk(n, row, weighted, last_row, last_weighted):
        source = origin(n)
        arrival(n).wait_recv()

        def rec(k, which):
            return got[source, k, pl.ds(which, 1), :]

        def emit(k, part, value):
            solved[source, k, pl.ds(part, 1), :] = value

        add_grid(last_weighted, last_row)
        work_chunk(rec, model_t[...], table_ref[...], row, weighted, emit, capacity, side)

        @pl.when(n > 0)
        def _():
            homeward(n).start()

    def two(step, carry):
        chunk(2 * step, row0, weighted0, row1, weighted1)
        chunk(2 * step + 1, row1, weighted1, row0, weighted0)
        return carry

    lax.fori_loop(0, owners // 2, two, 0)
    add_grid(weighted1, row1)
    grids[plane] = total[...].T.astype(jnp.bfloat16)

    def pass_on(which, half, to, sem):
        piece = grids.at[which] if half is None else grids.at[which, pl.ds(half * side, side)]
        return pltpu.make_async_remote_copy(
            src_ref=piece, dst_ref=piece, send_sem=grid_send.at[sem], recv_sem=grid_got.at[sem],
            device_id=(me, to), device_id_type=MESH,
        )

    started = [
        pass_on(plane, 0, ahead, 0),
        pass_on(plane, 1, behind, 1),
        pass_on(plane, 1, ahead, 2),
        pass_on(plane, 0, behind, 3),
        pass_on(plane, None, sibling, 6),
    ]
    for copy in started:
        copy.start()

    def came(which, half, sem):
        pass_on(which, half, sibling, sem).wait_recv()

    def onward(which, half, to, sem):
        copy = pass_on(which, half, to, sem)
        copy.start()
        started.append(copy)

    came(behind, 0, 0)
    onward(behind, 0, ahead, 4)
    came(ahead, 1, 1)
    onward(ahead, 1, behind, 5)

    def collect(n, carry):
        source = target(n)
        pltpu.make_async_remote_copy(
            src_ref=solved.at[source], dst_ref=returned.at[pl.ds(source * capacity, capacity)],
            send_sem=back_sem.at[source], recv_sem=home_sem.at[source], device_id=(source, plane), device_id_type=MESH,
        ).wait_recv()
        return carry

    lax.fori_loop(1, owners, collect, 0)
    returned[pl.ds(me * capacity, capacity)] = solved[me]

    def unpack(b, carry):
        residual_out[b] = returned[index_s[owners * capacity // lanes, b]]
        return carry

    lax.fori_loop(0, blocks, unpack, 0, unroll=8)

    came(behind, 1, 2)
    onward(behind, None, sibling, 7)
    came(ahead, 0, 3)
    onward(ahead, None, sibling, 8)
    came(opposite, 0, 4)
    came(opposite, 1, 5)
    onward(opposite, None, sibling, 9)

    def flip(which):
        return which + 1 - 2 * core

    acc = None
    for which, sem in ((plane, None), (behind, None), (ahead, None), (opposite, None), (sibling, 6), (flip(behind), 7), (flip(ahead), 8), (flip(opposite), 9)):
        if sem is not None:
            came(which, None, sem)
        term = coupling_s[plane, which] * grids[which].astype(jnp.float32)
        coupled_out[...] = term if acc is None else coupled_out[...] + term
        acc = True

    def settle(n, carry):
        outward(n).wait_send()
        homeward(n).wait_send()
        return carry

    lax.fori_loop(1, owners, settle, 0)
    for copy in started:
        copy.wait_send()


def body(visibilities, uv_cell, sub_pixel, w_plane, block_tile, model_grid, kernel_table, coupling):
    blocks = visibilities.shape[1]
    rows = visibilities.shape[3]
    owners = lax.axis_size("tile")
    capacity = 3 * blocks // owners
    tiles, side = model_grid.shape[1], model_grid.shape[2]
    oversample, support = kernel_table.shape[1], kernel_table.shape[2]
    planes = lax.axis_size("freq")
    chips_x, chips_y = planes // 2, 4
    table = kernel_table.reshape(-1, support).T.astype(jnp.float32)
    vmem = pl.BlockSpec(memory_space=pltpu.VMEM)
    smem = pl.BlockSpec(memory_space=pltpu.SMEM)
    copies = pltpu.SemaphoreType.DMA
    taps = (tiles * side, capacity * rows)
    residuals, coupled = pl.pallas_call(
        functools.partial(kernel, (owners, capacity, tiles, side, oversample, chips_y, chips_x)),
        out_shape=(
            jax.ShapeDtypeStruct((blocks, 2, rows), jnp.float32),
            jax.ShapeDtypeStruct((tiles * side, 2 * side), jnp.float32),
        ),
        in_specs=[smem] * 3 + [vmem] * 6,
        out_specs=[vmem] * 2,
        scratch_shapes=[
            pltpu.VMEM((blocks + 1, 4, rows), jnp.float32),
            pltpu.VMEM((4, rows), jnp.int32),
            pltpu.SMEM((4, rows), jnp.int32),
            pltpu.VMEM((2 * side, tiles * side), jnp.bfloat16),
            pltpu.VMEM((owners, capacity, 4, rows), jnp.float32),
            pltpu.VMEM((owners, capacity, 4, rows), jnp.float32),
            pltpu.VMEM((owners, capacity, 2, rows), jnp.float32),
            pltpu.VMEM((owners * capacity, 2, rows), jnp.float32),
            pltpu.VMEM(taps, jnp.bfloat16),
            pltpu.VMEM(taps, jnp.bfloat16),
            pltpu.VMEM(taps, jnp.bfloat16),
            pltpu.VMEM(taps, jnp.bfloat16),
            pltpu.VMEM((2 * side, tiles * side), jnp.float32),
            pltpu.VMEM((planes, tiles * side, 2 * side), jnp.bfloat16),
            copies,
            copies((owners,)),
            copies((owners,)),
            copies((owners,)),
            copies((owners,)),
            copies((10,)),
            copies((10,)),
        ],
        compiler_params=pltpu.CompilerParams(collective_id=0, has_side_effects=True, vmem_limit_bytes=32 << 20),
    )(
        block_tile,
        w_plane,
        coupling,
        block_tile,
        visibilities[0],
        uv_cell[0],
        sub_pixel[0],
        model_grid.reshape(tiles * side, 2 * side),
        table,
    )
    return residuals[None], coupled.reshape(1, tiles, side, 2 * side)


def solution(mesh):
    return jax.shard_map(
        body,
        mesh=mesh,
        in_specs=(
            P("freq", "tile", None, None),
            P("freq", "tile", None, None),
            P("freq", "tile", None, None),
            P("freq", "tile"),
            P("freq", "tile"),
            P("freq", "tile", None, None),
            P(),
            P(),
        ),
        out_specs=(P("freq", "tile", None, None), P("freq", "tile", None, None)),
        check_vma=False,
    )
```

```python
import functools

import jax
import jax.numpy as jnp
from jax import lax
from jax.experimental import pallas as pl
from jax.experimental.pallas import tpu as pltpu
from jax.sharding import PartitionSpec as P

SHIFT = 65536


def spread(start, table_row, table, lanes):
    sub = lax.broadcasted_iota(jnp.int32, (8, lanes), 0)
    taps = jnp.take_along_axis(table, jnp.broadcast_to(table_row, (8, lanes)), axis=1, mode="promise_in_bounds")
    offset = sub - start
    folded = jnp.take_along_axis(taps, jnp.bitwise_and(offset, 7), axis=0, mode="promise_in_bounds")
    return folded, lax.shift_right_arithmetic(offset, 3)


def twice(folded, group):
    values = jnp.concatenate([folded, folded], axis=0).astype(jnp.bfloat16)
    groups = jnp.concatenate([group, group + 1], axis=0).astype(jnp.float32).astype(jnp.bfloat16)
    return values, groups


def work_chunk(rec, model_t, table, row_ref, weighted_ref, emit, capacity, side):
    lanes = 128
    zero16 = jnp.zeros((16, lanes), jnp.bfloat16)
    column = []
    for k in range(capacity):
        position = rec(k, 2).astype(jnp.int32)
        lookup = rec(k, 3).astype(jnp.int32)
        folded, group = spread(lax.shift_right_logical(position, 16), lax.shift_right_logical(lookup, 16), table, lanes)
        values, groups = twice(folded, group)
        for tile in range(2 * side // 16):
            row_ref[pl.ds(16 * tile, 16), pl.ds(k * lanes, lanes)] = jnp.where(
                groups == jnp.bfloat16(-2 * tile), values, zero16
            )
        column.append(
            spread(jnp.bitwise_and(position, SHIFT - 1), jnp.bitwise_and(lookup, SHIFT - 1), table, lanes)
        )
    for pair in range(capacity // 2):
        partial = jnp.dot(
            model_t, row_ref[:, pl.ds(pair * 2 * lanes, 2 * lanes)], preferred_element_type=jnp.float32
        )
        for half in range(2):
            k = 2 * pair + half
            folded, group = column[k]
            block = partial[:, half * lanes : (half + 1) * lanes]
            picked = [jnp.zeros((8, lanes), jnp.float32)] * 2
            for tile in range(side // 8):
                hit = group == -tile
                for part in range(2):
                    start = part * side + 8 * tile
                    picked[part] = jnp.where(hit, block[start : start + 8], picked[part])
            for part in range(2):
                residual = rec(k, part) - jnp.sum(picked[part] * folded, axis=0, keepdims=True)
                emit(k, part, residual)
                values, groups = twice(residual * folded, group)
                for tile in range(side // 16):
                    weighted_ref[pl.ds(part * side + 16 * tile, 16), pl.ds(k * lanes, lanes)] = jnp.where(
                        groups == jnp.bfloat16(-2 * tile), values, zero16
                    )


MESH = pl.DeviceIdType.MESH


def kernel(
    dims,
    tile_h, plane_h, coupling_h, samples_h, cells_h, offsets_h, model_h, table_h,
    residual_out, coupled_out,
    tile_s, plane_s, tile_v, coupling_v, samples, cells, offsets, model, table_raw, table_ref,
    records, index_v, index_s, model_t, send, got, solved, returned, relayed, rehomed,
    row0, row1, weighted0, weighted1, total, grids,
    load_sem, index_sem, send_sem, got_sem, back_sem, home_sem, grid_send, grid_got,
    relay_send, relay_got, relay_on, rehome_send, rehome_got, rehome_on,
):
    owners, capacity, tiles, side, oversample, chips_y, chips_x = dims
    chips_z = owners // chips_y
    half_z, quarter_z = chips_z // 2, chips_z // 4
    blocks = samples.shape[0]
    lanes = 128
    me = lax.axis_index("tile")
    plane = lax.axis_index("freq")
    mine_y, mine_z = me // chips_z, lax.rem(me, chips_z)
    mine_x, core = plane // 2, lax.rem(plane, 2)
    far_group = chips_z - 3
    relays = [(far_group * chips_y + across, across) for across in range(1, 1)]

    def place(y, z):
        return lax.rem(mine_y + y + chips_y, chips_y) * chips_z + lax.rem(mine_z + z + chips_z, chips_z)

    def hop(n):
        group, across = n // chips_y, lax.rem(n, chips_y)
        past = group // (far_group + 1)
        far = group // far_group - past
        turn = group - past
        near = (turn + 1) // 2 * (2 * lax.rem(turn, 2) - 1)
        return across, near * (1 - far) + half_z * far

    def target(n):
        across, along = hop(n)
        return place(across, along)

    def origin(n):
        across, along = hop(n)
        return place(-across, -along)

    sibling = 2 * mine_x + 1 - core
    ahead = 2 * lax.rem(mine_x + 1, chips_x) + core
    behind = 2 * lax.rem(mine_x + chips_x - 1, chips_x) + core
    opposite = 2 * lax.rem(mine_x + 2, chips_x) + core

    loads = [
        pltpu.make_async_copy(source, to, load_sem.at[i])
        for i, (source, to) in enumerate(
            (
                (tile_h, tile_v),
                (tile_h, tile_s),
                (plane_h, plane_s),
                (cells_h, cells),
                (offsets_h, offsets),
                (samples_h, samples),
                (table_h, table_raw),
                (model_h, model),
                (coupling_h, coupling_v),
            )
        )
    ]
    for load in loads:
        load.start()

    barrier = pltpu.get_barrier_semaphore()

    def greet(n, carry):
        pl.semaphore_signal(barrier, inc=1, device_id=(target(n), plane), device_id_type=MESH)
        return carry

    lax.fori_loop(1, owners, greet, 0)
    for other in (sibling, ahead, behind):
        pl.semaphore_signal(barrier, inc=1, device_id=(me, other), device_id_type=MESH)

    loads[0].wait()
    owner = lax.shift_right_logical(tile_v[...], tiles.bit_length() - 1)
    wide = (blocks, lanes)
    down = lax.broadcasted_iota(jnp.int32, wide, 0)
    over = lax.broadcasted_iota(jnp.int32, wide, 1)

    def stand(row):
        return jnp.broadcast_to(row.astype(jnp.float32), wide).T.astype(jnp.int32)

    same = (stand(owner) == owner) & (down < over)
    slot = owner * capacity + jnp.sum(same.astype(jnp.int32), axis=0, keepdims=True)
    slots = stand(slot)
    for part in range(owners * capacity // lanes):
        index_v[pl.ds(part, 1), :] = blocks + jnp.sum(
            jnp.where(slots == over + part * lanes, down - blocks, 0), axis=0, keepdims=True
        )
    index_v[pl.ds(owners * capacity // lanes, 1), :] = slot
    index_copy = pltpu.make_async_copy(index_v, index_s, index_sem)
    index_copy.start()
    for load in loads[1:6]:
        load.wait()

    def fill(b, carry):
        tile = lax.rem(tile_s[0, b], tiles)
        kernel_plane = plane_s[0, b]
        records[b, pl.ds(0, 2), :] = samples[b]
        spot = (cells[b, pl.ds(0, 1), :] + tile * side) * SHIFT + cells[b, pl.ds(1, 1), :]
        lookup = offsets[b] * (lanes // oversample) + kernel_plane
        records[b, pl.ds(2, 1), :] = spot.astype(jnp.float32)
        records[b, pl.ds(3, 1), :] = (lookup[0:1] * SHIFT + lookup[1:2]).astype(jnp.float32)
        return carry

    lax.fori_loop(0, blocks, fill, 0, unroll=8)
    records[blocks] = jnp.where(
        lax.broadcasted_iota(jnp.int32, (4, lanes), 0) == 2, jnp.float32(tiles * side * SHIFT), jnp.float32(0)
    )
    index_copy.wait()

    def pack(to, carry):
        for j in range(capacity):
            s = to * capacity + j
            send[to, j] = records[index_s[s // lanes, lax.rem(s, lanes)]]
        return carry

    lax.fori_loop(0, owners, pack, 0)
    own = pltpu.make_async_copy(send.at[me], got.at[me], got_sem.at[me])
    own.start()
    pl.semaphore_wait(barrier, owners + 2)

    def each_direct(act):
        def visit(n, carry):
            direct = n > 0
            for relay, _ in relays:
                direct = direct & (n != relay)

            @pl.when(direct)
            def _():
                act(n)

            return carry

        lax.fori_loop(1, owners, visit, 0)

    def outward(n):
        to = target(n)
        return pltpu.make_async_remote_copy(
            src_ref=send.at[to], dst_ref=got.at[me], send_sem=send_sem.at[to], recv_sem=got_sem.at[me],
            device_id=(to, plane), device_id_type=MESH,
        )

    def arrival(n):
        source = origin(n)
        return pltpu.make_async_remote_copy(
            src_ref=send.at[source], dst_ref=got.at[source], send_sem=send_sem.at[source],
            recv_sem=got_sem.at[source], device_id=(source, plane), device_id_type=MESH,
        )

    def homeward(n):
        to = origin(n)
        return pltpu.make_async_remote_copy(
            src_ref=solved.at[to], dst_ref=returned.at[pl.ds(me * capacity, capacity)],
            send_sem=back_sem.at[to], recv_sem=home_sem.at[me], device_id=(to, plane), device_id_type=MESH,
        )

    def relay_out(i):
        return pltpu.make_async_remote_copy(
            src_ref=send.at[place(relays[i][1], half_z)], dst_ref=relayed.at[i], send_sem=relay_send.at[i],
            recv_sem=relay_got.at[i], device_id=(place(0, -quarter_z), plane), device_id_type=MESH,
        )

    def relay_onward(i):
        source = place(0, quarter_z)
        return pltpu.make_async_remote_copy(
            src_ref=relayed.at[i], dst_ref=got.at[source], send_sem=relay_on.at[i], recv_sem=got_sem.at[source],
            device_id=(place(relays[i][1], -quarter_z), plane), device_id_type=MESH,
        )

    def rehome_out(i):
        return pltpu.make_async_remote_copy(
            src_ref=solved.at[place(-relays[i][1], half_z)], dst_ref=rehomed.at[i], send_sem=rehome_send.at[i],
            recv_sem=rehome_got.at[i], device_id=(place(0, -quarter_z), plane), device_id_type=MESH,
        )

    def rehome_onward(i):
        keeper = place(0, quarter_z)
        return pltpu.make_async_remote_copy(
            src_ref=rehomed.at[i], dst_ref=returned.at[pl.ds(keeper * capacity, capacity)],
            send_sem=rehome_on.at[i], recv_sem=home_sem.at[keeper],
            device_id=(place(-relays[i][1], -quarter_z), plane), device_id_type=MESH,
        )

    for i in range(len(relays)):
        relay_out(i).start()
    each_direct(lambda n: outward(n).start())
    for load in loads[6:]:
        load.wait()
    for which in range(oversample):
        table_ref[:, pl.ds(which * (lanes // oversample), lanes // oversample)] = table_raw[which].astype(jnp.float32)
    model_t[...] = model[...].T
    total[...] = jnp.zeros_like(total)
    row1[...] = jnp.zeros_like(row1)
    weighted1[...] = jnp.zeros_like(weighted1)

    def add_grid(weighted, row):
        total[...] += lax.dot_general(
            weighted[...], row[...], (((1,), (1,)), ((), ())), preferred_element_type=jnp.float32
        )

    def chunk(n, row, weighted, last_row, last_weighted):
        source = origin(n)
        arrival(n).wait_recv()

        def rec(k, which):
            return got[source, k, pl.ds(which, 1), :]

        def emit(k, part, value):
            solved[source, k, pl.ds(part, 1), :] = value

        add_grid(last_weighted, last_row)
        work_chunk(rec, model_t[...], table_ref[...], row, weighted, emit, capacity, side)
        direct = n > 0
        for i, (relay, _) in enumerate(relays):
            direct = direct & (n != relay)

            @pl.when(n == relay)
            def _(i=i):
                rehome_out(i).start()

        @pl.when(direct)
        def _():
            homeward(n).start()

    def two(step, carry):
        @pl.when(step == 2)
        def _():
            for i in range(len(relays)):
                relay_out(i).wait_recv()
                relay_onward(i).start()

        @pl.when(step == owners // 2 - 2)
        def _():
            for i in range(len(relays)):
                rehome_out(i).wait_recv()
                rehome_onward(i).start()

        chunk(2 * step, row0, weighted0, row1, weighted1)
        chunk(2 * step + 1, row1, weighted1, row0, weighted0)
        return carry

    lax.fori_loop(0, owners // 2, two, 0)
    add_grid(weighted1, row1)
    grids[plane] = total[...].T.astype(jnp.bfloat16)

    def pass_on(which, half, to, sem):
        piece = grids.at[which] if half is None else grids.at[which, pl.ds(half * side, side)]
        return pltpu.make_async_remote_copy(
            src_ref=piece, dst_ref=piece, send_sem=grid_send.at[sem], recv_sem=grid_got.at[sem],
            device_id=(me, to), device_id_type=MESH,
        )

    started = [
        pass_on(plane, 0, ahead, 0),
        pass_on(plane, 1, behind, 1),
        pass_on(plane, 1, ahead, 2),
        pass_on(plane, 0, behind, 3),
        pass_on(plane, None, sibling, 6),
    ]
    for copy in started:
        copy.start()

    def came(which, half, sem):
        pass_on(which, half, sibling, sem).wait_recv()

    def onward(which, half, to, sem):
        copy = pass_on(which, half, to, sem)
        copy.start()
        started.append(copy)

    came(behind, 0, 0)
    onward(behind, 0, ahead, 4)
    came(ahead, 1, 1)
    onward(ahead, 1, behind, 5)

    def collect(n, carry):
        source = target(n)
        pltpu.make_async_remote_copy(
            src_ref=solved.at[source], dst_ref=returned.at[pl.ds(source * capacity, capacity)],
            send_sem=back_sem.at[source], recv_sem=home_sem.at[source], device_id=(source, plane), device_id_type=MESH,
        ).wait_recv()
        return carry

    lax.fori_loop(1, owners, collect, 0)
    returned[pl.ds(me * capacity, capacity)] = solved[me]

    def unpack(b, carry):
        residual_out[b] = returned[index_s[owners * capacity // lanes, b]]
        return carry

    lax.fori_loop(0, blocks, unpack, 0, unroll=8)

    came(behind, 1, 2)
    onward(behind, None, sibling, 7)
    came(ahead, 0, 3)
    onward(ahead, None, sibling, 8)
    came(opposite, 0, 4)
    came(opposite, 1, 5)
    onward(opposite, None, sibling, 9)

    def flip(which):
        return which + 1 - 2 * core

    share = coupling_v[pl.ds(plane, 1), :]
    number = lax.broadcasted_iota(jnp.int32, share.shape, 1)

    def term(which):
        part = jnp.sum(jnp.where(number == which, share, 0.0), axis=1, keepdims=True)
        return part * grids[which].astype(jnp.float32)

    coupled_out[...] = term(plane) + term(behind) + term(ahead) + term(opposite)
    for which, sem in ((sibling, 6), (flip(behind), 7), (flip(ahead), 8), (flip(opposite), 9)):
        came(which, None, sem)
    coupled_out[...] += term(sibling) + term(flip(behind)) + term(flip(ahead)) + term(flip(opposite))

    def settle(n):
        outward(n).wait_send()
        homeward(n).wait_send()

    each_direct(settle)
    for i in range(len(relays)):
        for copy in (relay_out(i), relay_onward(i), rehome_out(i), rehome_onward(i)):
            copy.wait_send()
    for copy in started:
        copy.wait_send()


def body(visibilities, uv_cell, sub_pixel, w_plane, block_tile, model_grid, kernel_table, coupling):
    blocks = visibilities.shape[1]
    rows = visibilities.shape[3]
    owners = lax.axis_size("tile")
    capacity = 3 * blocks // owners
    tiles, side = model_grid.shape[1], model_grid.shape[2]
    oversample = kernel_table.shape[1]
    planes = lax.axis_size("freq")
    chips_x, chips_y = planes // 2, 4
    vmem = pl.BlockSpec(memory_space=pltpu.VMEM)
    hbm = pl.BlockSpec(memory_space=pltpu.HBM)
    copies = pltpu.SemaphoreType.DMA
    taps = (tiles * side, capacity * rows)
    operands = (
        block_tile,
        w_plane,
        coupling,
        visibilities[0],
        uv_cell[0],
        sub_pixel[0],
        model_grid.reshape(tiles * side, 2 * side),
        kernel_table.transpose(1, 2, 0),
    )
    residuals, coupled = pl.pallas_call(
        functools.partial(kernel, (owners, capacity, tiles, side, oversample, chips_y, chips_x)),
        out_shape=(
            jax.ShapeDtypeStruct((blocks, 2, rows), jnp.float32),
            jax.ShapeDtypeStruct((tiles * side, 2 * side), jnp.float32),
        ),
        in_specs=[hbm] * len(operands),
        out_specs=[vmem] * 2,
        scratch_shapes=[
            pltpu.SMEM((1, blocks), jnp.int32),
            pltpu.SMEM((1, blocks), jnp.int32),
            pltpu.VMEM((1, blocks), jnp.int32),
            pltpu.VMEM((planes, planes), jnp.float32),
            pltpu.VMEM((blocks, 2, rows), jnp.float32),
            pltpu.VMEM((blocks, 2, rows), jnp.int32),
            pltpu.VMEM((blocks, 2, rows), jnp.int32),
            pltpu.VMEM((tiles * side, 2 * side), jnp.bfloat16),
            pltpu.VMEM(operands[-1].shape, jnp.bfloat16),
            pltpu.VMEM((8, rows), jnp.float32),
            pltpu.VMEM((blocks + 1, 4, rows), jnp.float32),
            pltpu.VMEM((4, rows), jnp.int32),
            pltpu.SMEM((4, rows), jnp.int32),
            pltpu.VMEM((2 * side, tiles * side), jnp.bfloat16),
            pltpu.VMEM((owners, capacity, 4, rows), jnp.float32),
            pltpu.VMEM((owners, capacity, 4, rows), jnp.float32),
            pltpu.VMEM((owners, capacity, 2, rows), jnp.float32),
            pltpu.VMEM((owners * capacity, 2, rows), jnp.float32),
            pltpu.VMEM((2, capacity, 4, rows), jnp.float32),
            pltpu.VMEM((2, capacity, 2, rows), jnp.float32),
            pltpu.VMEM(taps, jnp.bfloat16),
            pltpu.VMEM(taps, jnp.bfloat16),
            pltpu.VMEM(taps, jnp.bfloat16),
            pltpu.VMEM(taps, jnp.bfloat16),
            pltpu.VMEM((2 * side, tiles * side), jnp.float32),
            pltpu.VMEM((planes, tiles * side, 2 * side), jnp.bfloat16),
            copies((len(operands) + 1,)),
            copies,
            copies((owners,)),
            copies((owners,)),
            copies((owners,)),
            copies((owners,)),
            copies((10,)),
            copies((10,)),
            copies((2,)),
            copies((2,)),
            copies((2,)),
            copies((2,)),
            copies((2,)),
            copies((2,)),
        ],
        compiler_params=pltpu.CompilerParams(collective_id=0, has_side_effects=True, vmem_limit_bytes=40 << 20),
    )(*(pltpu.with_memory_space_constraint(operand, pltpu.HBM) for operand in operands))
    return residuals[None], coupled.reshape(1, tiles, side, 2 * side)


def solution(mesh):
    return jax.shard_map(
        body,
        mesh=mesh,
        in_specs=(
            P("freq", "tile", None, None),
            P("freq", "tile", None, None),
            P("freq", "tile", None, None),
            P("freq", "tile"),
            P("freq", "tile"),
            P("freq", "tile", None, None),
            P(),
            P(),
        ),
        out_specs=(P("freq", "tile", None, None), P("freq", "tile", None, None)),
        check_vma=False,
    )
```

```python
import functools

import jax
import jax.numpy as jnp
from jax import lax
from jax.experimental import pallas as pl
from jax.experimental.pallas import tpu as pltpu
from jax.sharding import PartitionSpec as P

SHIFT = 65536
LEVELS = 32767.0
PIECES = 4
SAMPLE_FRACTION = 2.0**24
MODEL_FRACTION = 2.0**23


def spread(start, table_row, table, lanes):
    sub = lax.broadcasted_iota(jnp.int32, (8, lanes), 0)
    taps = jnp.take_along_axis(table, jnp.broadcast_to(table_row, (8, lanes)), axis=1, mode="promise_in_bounds")
    offset = sub - start
    folded = jnp.take_along_axis(taps, jnp.bitwise_and(offset, 7), axis=0, mode="promise_in_bounds")
    return folded, lax.shift_right_arithmetic(offset, 3)


def twice(folded, group):
    values = jnp.concatenate([folded, folded], axis=0).astype(jnp.bfloat16)
    groups = jnp.concatenate([group, group + 1], axis=0).astype(jnp.float32).astype(jnp.bfloat16)
    return values, groups


def measure(values, fraction):
    while values.ndim > 2:
        values = jnp.max(values, axis=0)
    return jnp.floor(jnp.max(values, keepdims=True) * fraction).astype(jnp.int32) + 1


def encode(first, second, gain):
    high, low = (jnp.floor(value * gain + 0.5).astype(jnp.int32) for value in (first, second))
    return lax.shift_left(high, 16) | jnp.bitwise_and(low, SHIFT - 1)


def decode(word, scale, fraction):
    gain = scale.astype(jnp.float32) * (1.0 / (LEVELS * fraction))
    high = lax.shift_right_arithmetic(word, 16)
    low = lax.shift_right_arithmetic(lax.shift_left(word, 16), 16)
    return high.astype(jnp.float32) * gain, low.astype(jnp.float32) * gain


def work_chunk(message, model_t, table, row_ref, weighted_ref, model_ref, capacity, side):
    lanes = 128
    zero16 = jnp.zeros((16, lanes), jnp.bfloat16)
    samples = decode(message[pl.ds(0, capacity), :], message[pl.ds(3 * capacity, 1), :], SAMPLE_FRACTION)
    column = []
    for k in range(capacity):
        position = message[pl.ds(capacity + k, 1), :]
        lookup = message[pl.ds(2 * capacity + k, 1), :]
        folded, group = spread(lax.shift_right_logical(position, 16), lax.shift_right_logical(lookup, 16), table, lanes)
        values, groups = twice(folded, group)
        for tile in range(2 * side // 16):
            row_ref[pl.ds(16 * tile, 16), pl.ds(k * lanes, lanes)] = jnp.where(
                groups == jnp.bfloat16(-2 * tile), values, zero16
            )
        column.append(
            spread(jnp.bitwise_and(position, SHIFT - 1), jnp.bitwise_and(lookup, SHIFT - 1), table, lanes)
        )
    for pair in range(capacity // 2):
        partial = jnp.dot(
            model_t, row_ref[:, pl.ds(pair * 2 * lanes, 2 * lanes)], preferred_element_type=jnp.float32
        )
        for half in range(2):
            k = 2 * pair + half
            folded, group = column[k]
            block = partial[:, half * lanes : (half + 1) * lanes]
            picked = [jnp.zeros((8, lanes), jnp.float32)] * 2
            for tile in range(side // 8):
                hit = group == -tile
                for part in range(2):
                    start = part * side + 8 * tile
                    picked[part] = jnp.where(hit, block[start : start + 8], picked[part])
            for part in range(2):
                degridded = jnp.sum(picked[part] * folded, axis=0, keepdims=True)
                model_ref[pl.ds(part * 16 + k, 1), :] = degridded
                residual = samples[part][k : k + 1] - degridded
                values, groups = twice(residual * folded, group)
                for tile in range(side // 16):
                    weighted_ref[pl.ds(part * side + 16 * tile, 16), pl.ds(k * lanes, lanes)] = jnp.where(
                        groups == jnp.bfloat16(-2 * tile), values, zero16
                    )


MESH = pl.DeviceIdType.MESH


def kernel(
    dims,
    tile_h, plane_h, coupling_h, samples_h, cells_h, offsets_h, model_h, table_h,
    residual_out, coupled_out,
    tile_s, plane_s, tile_v, coupling_v, samples, cells, offsets, model, table_raw, table_ref,
    records, index_v, index_s, modelled, model_t, send, got, solved, returned,
    row0, row1, weighted0, weighted1, total, grids,
    load_sem, index_sem, send_sem, got_sem, back_sem, home_sem, grid_send, grid_got,
):
    owners, capacity, tiles, side, oversample, chips_y, chips_x = dims
    chips_z = owners // chips_y
    half_z = chips_z // 2
    blocks = samples_h.shape[0]
    lanes = 128
    out_rows, back_rows = 3 * capacity + 1, capacity + 1
    me = lax.axis_index("tile")
    plane = lax.axis_index("freq")
    mine_y, mine_z = me // chips_z, lax.rem(me, chips_z)
    mine_x, core = plane // 2, lax.rem(plane, 2)
    far_group = chips_z - 3

    def place(y, z):
        return lax.rem(mine_y + y + chips_y, chips_y) * chips_z + lax.rem(mine_z + z + chips_z, chips_z)

    def hop(n):
        group, across = n // chips_y, lax.rem(n, chips_y)
        past = group // (far_group + 1)
        far = group // far_group - past
        turn = group - past
        near = (turn + 1) // 2 * (2 * lax.rem(turn, 2) - 1)
        return across, near * (1 - far) + half_z * far

    def target(n):
        across, along = hop(n)
        return place(across, along)

    def origin(n):
        across, along = hop(n)
        return place(-across, -along)

    sibling = 2 * mine_x + 1 - core
    ahead = 2 * lax.rem(mine_x + 1, chips_x) + core
    behind = 2 * lax.rem(mine_x + chips_x - 1, chips_x) + core
    opposite = 2 * lax.rem(mine_x + 2, chips_x) + core

    loads = [
        pltpu.make_async_copy(source, to, load_sem.at[i])
        for i, (source, to) in enumerate(
            (
                (tile_h, tile_v),
                (tile_h, tile_s),
                (plane_h, plane_s),
                (cells_h, cells),
                (offsets_h, offsets),
                (samples_h, samples),
                (table_h, table_raw),
                (model_h, model),
                (coupling_h, coupling_v),
            )
        )
    ]
    for load in loads:
        load.start()

    barrier = pltpu.get_barrier_semaphore()

    def greet(n, carry):
        pl.semaphore_signal(barrier, inc=1, device_id=(target(n), plane), device_id_type=MESH)
        return carry

    lax.fori_loop(1, owners, greet, 0)
    for other in (sibling, ahead, behind):
        pl.semaphore_signal(barrier, inc=1, device_id=(me, other), device_id_type=MESH)

    loads[0].wait()
    owner = lax.shift_right_logical(tile_v[...], tiles.bit_length() - 1)
    wide = (blocks, lanes)
    down = lax.broadcasted_iota(jnp.int32, wide, 0)
    over = lax.broadcasted_iota(jnp.int32, wide, 1)

    def stand(row):
        return jnp.broadcast_to(row.astype(jnp.float32), wide).T.astype(jnp.int32)

    same = (stand(owner) == owner) & (down < over)
    slot = owner * capacity + jnp.sum(same.astype(jnp.int32), axis=0, keepdims=True)
    slots = stand(slot)
    for part in range(owners * capacity // lanes):
        index_v[pl.ds(part, 1), :] = blocks + jnp.sum(
            jnp.where(slots == over + part * lanes, down - blocks, 0), axis=0, keepdims=True
        )
    index_v[pl.ds(3, 1), :] = owner
    index_v[pl.ds(5, 3), :] = jnp.zeros((3, lanes), jnp.int32)
    index_v[pl.ds(4, 1), :] = slot - owner * capacity
    index_copy = pltpu.make_async_copy(index_v, index_s, index_sem)
    index_copy.start()
    for load in loads[1:6]:
        load.wait()

    scale = measure(jnp.abs(samples[...]), SAMPLE_FRACTION)
    gain = (LEVELS * SAMPLE_FRACTION) / scale.astype(jnp.float32)
    scale_row = jnp.broadcast_to(scale, (1, lanes))

    def fill(b, carry):
        tile = lax.rem(tile_s[0, b], tiles)
        kernel_plane = plane_s[0, b]
        spot = (cells[b, pl.ds(0, 1), :] + tile * side) * SHIFT + cells[b, pl.ds(1, 1), :]
        lookup = offsets[b] * (lanes // oversample) + kernel_plane
        records[b, pl.ds(0, 1), :] = encode(samples[b, pl.ds(0, 1), :], samples[b, pl.ds(1, 1), :], gain)
        records[b, pl.ds(1, 1), :] = spot
        records[b, pl.ds(2, 1), :] = lookup[0:1] * SHIFT + lookup[1:2]
        return carry

    lax.fori_loop(0, blocks, fill, 0, unroll=8)
    records[blocks, pl.ds(0, 3), :] = jnp.where(
        lax.broadcasted_iota(jnp.int32, (3, lanes), 0) == 1, tiles * side * SHIFT, 0
    )
    index_copy.wait()

    def outgoing(to):
        return send.at[to, pl.ds(0, out_rows)]

    def incoming(source):
        return got.at[source, pl.ds(0, out_rows)]

    def pack(to, carry):
        for j in range(capacity):
            s = to * capacity + j
            source = index_s[s // lanes, lax.rem(s, lanes)]
            send[to, pl.ds(j, 3, stride=capacity), :] = records[source, pl.ds(0, 3), :]
        send[to, pl.ds(3 * capacity, 1), :] = scale_row
        return carry

    lax.fori_loop(0, owners, pack, 0)
    own = pltpu.make_async_copy(outgoing(me), incoming(me), got_sem.at[me])
    own.start()
    pl.semaphore_wait(barrier, owners + 2)

    def each_partner(act):
        def visit(n, carry):
            act(n)
            return carry

        lax.fori_loop(1, owners, visit, 0)

    def outward(n):
        to = target(n)
        return pltpu.make_async_remote_copy(
            src_ref=outgoing(to), dst_ref=incoming(me), send_sem=send_sem.at[to], recv_sem=got_sem.at[me],
            device_id=(to, plane), device_id_type=MESH,
        )

    def arrival(n):
        source = origin(n)
        return pltpu.make_async_remote_copy(
            src_ref=outgoing(source), dst_ref=incoming(source), send_sem=send_sem.at[source],
            recv_sem=got_sem.at[source], device_id=(source, plane), device_id_type=MESH,
        )

    def homeward(n):
        to = origin(n)
        return pltpu.make_async_remote_copy(
            src_ref=solved.at[to, pl.ds(0, back_rows)], dst_ref=returned.at[me, pl.ds(0, back_rows)],
            send_sem=back_sem.at[to], recv_sem=home_sem.at[me], device_id=(to, plane), device_id_type=MESH,
        )

    each_partner(lambda n: outward(n).start())
    for load in loads[6:]:
        load.wait()
    for which in range(oversample):
        table_ref[:, pl.ds(which * (lanes // oversample), lanes // oversample)] = table_raw[which].astype(jnp.float32)
    model_t[...] = model[...].T
    total[...] = jnp.zeros_like(total)
    row1[...] = jnp.zeros_like(row1)
    weighted1[...] = jnp.zeros_like(weighted1)

    def add_grid(weighted, row):
        total[...] += lax.dot_general(
            row[...], weighted[...], (((1,), (1,)), ((), ())), preferred_element_type=jnp.float32
        )

    def chunk(n, turn, row, weighted, last_row, last_weighted):
        source = origin(n)
        add_grid(last_weighted, last_row)
        work_chunk(got.at[source], model_t[...], table_ref[...], row, weighted, modelled.at[turn], capacity, side)
        real, imaginary = modelled[turn, pl.ds(0, capacity), :], modelled[turn, pl.ds(16, capacity), :]
        here = measure(jnp.maximum(jnp.abs(real), jnp.abs(imaginary)), MODEL_FRACTION)
        solved[source, pl.ds(0, capacity), :] = encode(
            real, imaginary, (LEVELS * MODEL_FRACTION) / here.astype(jnp.float32)
        )
        solved[source, pl.ds(capacity, 1), :] = jnp.broadcast_to(here, (1, lanes))

    def group(step, carry):
        first = chips_y * step
        for across in range(chips_y):
            arrival(first + across).wait_recv()
        for across in range(0, chips_y, 2):
            chunk(first + across, across, row0, weighted0, row1, weighted1)
            chunk(first + across + 1, across + 1, row1, weighted1, row0, weighted0)

        @pl.when(step > 0)
        def _():
            homeward(first).start()

        for across in range(1, chips_y):
            homeward(first + across).start()
        return carry

    lax.fori_loop(0, chips_z, group, 0)
    add_grid(weighted1, row1)

    piece_rows = tiles * side // PIECES
    half = PIECES // 2

    def pass_on(which, piece, to, route):
        part = grids.at[which, pl.ds(piece * piece_rows, piece_rows)]
        return pltpu.make_async_remote_copy(
            src_ref=part, dst_ref=part, send_sem=grid_send.at[route, piece], recv_sem=grid_got.at[route, piece],
            device_id=(me, to), device_id_type=MESH,
        )

    started = []

    def launch(which, piece, to, route):
        copy = pass_on(which, piece, to, route)
        copy.start()
        started.append(copy)

    def came(which, piece, route):
        pass_on(which, piece, sibling, route).wait_recv()

    for piece in range(PIECES):
        spot = pl.ds(piece * piece_rows, piece_rows)
        grids[plane, spot, :] = total[spot, :].astype(jnp.bfloat16)
    for piece in range(PIECES):
        launch(plane, piece, ahead, 0)
        launch(plane, PIECES - 1 - piece, behind, 1)
    for piece in range(PIECES):
        launch(plane, piece, sibling, 4)
    for turn in range(PIECES):
        other = PIECES - 1 - turn
        came(behind, turn, 0)
        if turn < half:
            launch(behind, turn, ahead, 2)
        came(ahead, other, 1)
        if turn < half:
            launch(ahead, other, behind, 3)
        launch(behind, turn, sibling, 5)
        launch(ahead, other, sibling, 6)

    def collect(n, carry):
        source = target(n)
        pltpu.make_async_remote_copy(
            src_ref=solved.at[source, pl.ds(0, back_rows)], dst_ref=returned.at[source, pl.ds(0, back_rows)],
            send_sem=back_sem.at[source], recv_sem=home_sem.at[source], device_id=(source, plane), device_id_type=MESH,
        ).wait_recv()
        return carry

    lax.fori_loop(1, owners, collect, 0)
    returned[me, pl.ds(0, back_rows)] = solved[me, pl.ds(0, back_rows)]

    def unpack(b, carry):
        keeper = index_s[3, b]
        model_here = decode(
            returned[keeper, pl.ds(index_s[4, b], 1), :], returned[keeper, pl.ds(capacity, 1), :], MODEL_FRACTION
        )
        for part in range(2):
            residual_out[b, pl.ds(part, 1), :] = samples[b, pl.ds(part, 1), :] - model_here[part]
        return carry

    lax.fori_loop(0, blocks, unpack, 0, unroll=8)

    for turn in range(half):
        other = PIECES - 1 - turn
        came(opposite, turn, 2)
        launch(opposite, turn, sibling, 7)
        came(opposite, other, 3)
        launch(opposite, other, sibling, 7)

    def flip(which):
        return which + 1 - 2 * core

    share = coupling_v[pl.ds(plane, 1), :]
    number = lax.broadcasted_iota(jnp.int32, share.shape, 1)

    def term(which):
        part = jnp.sum(jnp.where(number == which, share, 0.0), axis=1, keepdims=True)
        return part * grids[which].astype(jnp.float32)

    coupled_out[...] = term(plane) + term(behind) + term(ahead) + term(opposite)
    for route, which in enumerate((sibling, flip(behind), flip(ahead), flip(opposite))):
        for piece in range(PIECES):
            came(which, piece, 4 + route)
    coupled_out[...] += term(sibling) + term(flip(behind)) + term(flip(ahead)) + term(flip(opposite))

    def settle(n):
        outward(n).wait_send()
        homeward(n).wait_send()

    each_partner(settle)
    for copy in started:
        copy.wait_send()


def body(visibilities, uv_cell, sub_pixel, w_plane, block_tile, model_grid, kernel_table, coupling):
    blocks = visibilities.shape[1]
    rows = visibilities.shape[3]
    owners = lax.axis_size("tile")
    capacity = 3 * blocks // owners
    tiles, side = model_grid.shape[1], model_grid.shape[2]
    oversample = kernel_table.shape[1]
    planes = lax.axis_size("freq")
    chips_x, chips_y = planes // 2, 4
    vmem = pl.BlockSpec(memory_space=pltpu.VMEM)
    hbm = pl.BlockSpec(memory_space=pltpu.HBM)
    copies = pltpu.SemaphoreType.DMA
    taps = (tiles * side, capacity * rows)
    operands = (
        block_tile,
        w_plane,
        coupling,
        visibilities[0],
        uv_cell[0],
        sub_pixel[0],
        model_grid.reshape(tiles * side, 2 * side),
        kernel_table.transpose(1, 2, 0),
    )
    residuals, coupled = pl.pallas_call(
        functools.partial(kernel, (owners, capacity, tiles, side, oversample, chips_y, chips_x)),
        out_shape=(
            jax.ShapeDtypeStruct((blocks, 2, rows), jnp.float32),
            jax.ShapeDtypeStruct((tiles * side, 2 * side), jnp.float32),
        ),
        in_specs=[hbm] * len(operands),
        out_specs=[vmem] * 2,
        scratch_shapes=[
            pltpu.SMEM((1, blocks), jnp.int32),
            pltpu.SMEM((1, blocks), jnp.int32),
            pltpu.VMEM((1, blocks), jnp.int32),
            pltpu.VMEM((planes, planes), jnp.float32),
            pltpu.VMEM((blocks, 2, rows), jnp.float32),
            pltpu.VMEM((blocks, 2, rows), jnp.int32),
            pltpu.VMEM((blocks, 2, rows), jnp.int32),
            pltpu.VMEM((tiles * side, 2 * side), jnp.bfloat16),
            pltpu.VMEM(operands[-1].shape, jnp.bfloat16),
            pltpu.VMEM((8, rows), jnp.float32),
            pltpu.VMEM((blocks + 1, 4, rows), jnp.int32),
            pltpu.VMEM((8, rows), jnp.int32),
            pltpu.SMEM((8, rows), jnp.int32),
            pltpu.VMEM((chips_y, 32, rows), jnp.float32),
            pltpu.VMEM((2 * side, tiles * side), jnp.bfloat16),
            pltpu.VMEM((owners, 40, rows), jnp.int32),
            pltpu.VMEM((owners, 40, rows), jnp.int32),
            pltpu.VMEM((owners, 16, rows), jnp.int32),
            pltpu.VMEM((owners, 16, rows), jnp.int32),
            pltpu.VMEM(taps, jnp.bfloat16),
            pltpu.VMEM(taps, jnp.bfloat16),
            pltpu.VMEM(taps, jnp.bfloat16),
            pltpu.VMEM(taps, jnp.bfloat16),
            pltpu.VMEM((tiles * side, 2 * side), jnp.float32),
            pltpu.VMEM((planes, tiles * side, 2 * side), jnp.bfloat16),
            copies((len(operands) + 1,)),
            copies,
            copies((owners,)),
            copies((owners,)),
            copies((owners,)),
            copies((owners,)),
            copies((8, PIECES)),
            copies((8, PIECES)),
        ],
        compiler_params=pltpu.CompilerParams(collective_id=0, has_side_effects=True, vmem_limit_bytes=40 << 20),
    )(*(pltpu.with_memory_space_constraint(operand, pltpu.HBM) for operand in operands))
    return residuals[None], coupled.reshape(1, tiles, side, 2 * side)


def solution(mesh):
    return jax.shard_map(
        body,
        mesh=mesh,
        in_specs=(
            P("freq", "tile", None, None),
            P("freq", "tile", None, None),
            P("freq", "tile", None, None),
            P("freq", "tile"),
            P("freq", "tile"),
            P("freq", "tile", None, None),
            P(),
            P(),
        ),
        out_specs=(P("freq", "tile", None, None), P("freq", "tile", None, None)),
        check_vma=False,
    )
```

```python
import functools

import jax
import jax.numpy as jnp
from jax import lax
from jax.experimental import pallas as pl
from jax.experimental.pallas import tpu as pltpu
from jax.sharding import PartitionSpec as P

SHIFT = 65536
LEVELS = 32767.0
PIECES = 4
SAMPLE_FRACTION = 2.0**24
MODEL_FRACTION = 2.0**23


def spread(start, table_row, table, lanes):
    sub = lax.broadcasted_iota(jnp.int32, (8, lanes), 0)
    taps = jnp.take_along_axis(table, jnp.broadcast_to(table_row, (8, lanes)), axis=1, mode="promise_in_bounds")
    offset = sub - start
    folded = jnp.take_along_axis(taps, jnp.bitwise_and(offset, 7), axis=0, mode="promise_in_bounds")
    return folded, lax.shift_right_arithmetic(offset, 3)


def twice(folded, group):
    values = jnp.concatenate([folded, folded], axis=0).astype(jnp.bfloat16)
    groups = jnp.concatenate([group, group + 1], axis=0).astype(jnp.float32).astype(jnp.bfloat16)
    return values, groups


def measure(values, fraction):
    while values.ndim > 2:
        values = jnp.max(values, axis=0)
    return jnp.floor(jnp.max(values, keepdims=True) * fraction).astype(jnp.int32) + 1


def encode(first, second, gain):
    high, low = (jnp.floor(value * gain + 0.5).astype(jnp.int32) for value in (first, second))
    return lax.shift_left(high, 16) | jnp.bitwise_and(low, SHIFT - 1)


def decode(word, scale, fraction):
    gain = scale.astype(jnp.float32) * (1.0 / (LEVELS * fraction))
    high = lax.shift_right_arithmetic(word, 16)
    low = lax.shift_right_arithmetic(lax.shift_left(word, 16), 16)
    return high.astype(jnp.float32) * gain, low.astype(jnp.float32) * gain


def work_chunk(message, model_t, table, row_ref, weighted_ref, model_ref, capacity, side):
    lanes = 128
    zero16 = jnp.zeros((16, lanes), jnp.bfloat16)
    samples = decode(message[pl.ds(0, capacity), :], message[pl.ds(3 * capacity, 1), :], SAMPLE_FRACTION)
    column = []
    for k in range(capacity):
        position = message[pl.ds(capacity + k, 1), :]
        lookup = message[pl.ds(2 * capacity + k, 1), :]
        folded, group = spread(lax.shift_right_logical(position, 16), lax.shift_right_logical(lookup, 16), table, lanes)
        values, groups = twice(folded, group)
        for tile in range(2 * side // 16):
            row_ref[pl.ds(16 * tile, 16), pl.ds(k * lanes, lanes)] = jnp.where(
                groups == jnp.bfloat16(-2 * tile), values, zero16
            )
        column.append(
            spread(jnp.bitwise_and(position, SHIFT - 1), jnp.bitwise_and(lookup, SHIFT - 1), table, lanes)
        )
    for pair in range(capacity // 2):
        partial = jnp.dot(
            model_t, row_ref[:, pl.ds(pair * 2 * lanes, 2 * lanes)], preferred_element_type=jnp.float32
        )
        for half in range(2):
            k = 2 * pair + half
            folded, group = column[k]
            block = partial[:, half * lanes : (half + 1) * lanes]
            picked = [jnp.zeros((8, lanes), jnp.float32)] * 2
            for tile in range(side // 8):
                hit = group == -tile
                for part in range(2):
                    start = part * side + 8 * tile
                    picked[part] = jnp.where(hit, block[start : start + 8], picked[part])
            for part in range(2):
                degridded = jnp.sum(picked[part] * folded, axis=0, keepdims=True)
                model_ref[pl.ds(part * 16 + k, 1), :] = degridded
                residual = samples[part][k : k + 1] - degridded
                values, groups = twice(residual * folded, group)
                for tile in range(side // 16):
                    weighted_ref[pl.ds(part * side + 16 * tile, 16), pl.ds(k * lanes, lanes)] = jnp.where(
                        groups == jnp.bfloat16(-2 * tile), values, zero16
                    )


MESH = pl.DeviceIdType.MESH


def kernel(
    dims,
    tile_h, plane_h, coupling_h, samples_h, cells_h, offsets_h, model_h, table_h,
    residual_out, coupled_out,
    tile_s, plane_s, tile_v, coupling_v, samples, cells, offsets, model, table_raw, table_ref,
    records, index_v, index_s, modelled, model_t, send, got, solved, returned,
    row0, row1, weighted0, weighted1, total, grids,
    load_sem, index_sem, send_sem, got_sem, back_sem, home_sem, grid_send, grid_got,
):
    owners, capacity, tiles, side, oversample, chips_y, chips_x = dims
    chips_z = owners // chips_y
    half_z = chips_z // 2
    blocks = samples_h.shape[0]
    lanes = 128
    out_rows, back_rows = 3 * capacity + 1, capacity + 1
    me = lax.axis_index("tile")
    plane = lax.axis_index("freq")
    mine_y, mine_z = me // chips_z, lax.rem(me, chips_z)
    mine_x, core = plane // 2, lax.rem(plane, 2)
    far_group = chips_z - 3

    def place(y, z):
        return lax.rem(mine_y + y + chips_y, chips_y) * chips_z + lax.rem(mine_z + z + chips_z, chips_z)

    def hop(n):
        group, across = n // chips_y, lax.rem(n, chips_y)
        past = group // (far_group + 1)
        far = group // far_group - past
        turn = group - past
        near = (turn + 1) // 2 * (2 * lax.rem(turn, 2) - 1)
        return across, near * (1 - far) + half_z * far

    def target(n):
        across, along = hop(n)
        return place(across, along)

    def origin(n):
        across, along = hop(n)
        return place(-across, -along)

    sibling = 2 * mine_x + 1 - core
    ahead = 2 * lax.rem(mine_x + 1, chips_x) + core
    behind = 2 * lax.rem(mine_x + chips_x - 1, chips_x) + core
    opposite = 2 * lax.rem(mine_x + 2, chips_x) + core

    loads = [
        pltpu.make_async_copy(source, to, load_sem.at[i])
        for i, (source, to) in enumerate(
            (
                (tile_h, tile_v),
                (tile_h, tile_s),
                (plane_h, plane_s),
                (cells_h, cells),
                (offsets_h, offsets),
                (samples_h, samples),
                (table_h, table_raw),
                (model_h, model),
                (coupling_h, coupling_v),
            )
        )
    ]
    for load in loads:
        load.start()

    barrier = pltpu.get_barrier_semaphore()

    def greet(n, carry):
        pl.semaphore_signal(barrier, inc=1, device_id=(target(n), plane), device_id_type=MESH)
        return carry

    lax.fori_loop(1, owners, greet, 0)
    for other in (sibling, ahead, behind):
        pl.semaphore_signal(barrier, inc=1, device_id=(me, other), device_id_type=MESH)

    loads[0].wait()
    owner = lax.shift_right_logical(tile_v[...], tiles.bit_length() - 1)
    wide = (blocks, lanes)
    down = lax.broadcasted_iota(jnp.int32, wide, 0)
    over = lax.broadcasted_iota(jnp.int32, wide, 1)

    def stand(row):
        return jnp.broadcast_to(row.astype(jnp.float32), wide).T.astype(jnp.int32)

    same = (stand(owner) == owner) & (down < over)
    slot = owner * capacity + jnp.sum(same.astype(jnp.int32), axis=0, keepdims=True)
    slots = stand(slot)
    for part in range(owners * capacity // lanes):
        index_v[pl.ds(part, 1), :] = blocks + jnp.sum(
            jnp.where(slots == over + part * lanes, down - blocks, 0), axis=0, keepdims=True
        )
    index_v[pl.ds(3, 1), :] = owner
    index_v[pl.ds(5, 3), :] = jnp.zeros((3, lanes), jnp.int32)
    index_v[pl.ds(4, 1), :] = slot - owner * capacity
    index_copy = pltpu.make_async_copy(index_v, index_s, index_sem)
    index_copy.start()
    for load in loads[1:6]:
        load.wait()

    scale = measure(jnp.abs(samples[...]), SAMPLE_FRACTION)
    gain = (LEVELS * SAMPLE_FRACTION) / scale.astype(jnp.float32)
    scale_row = jnp.broadcast_to(scale, (1, lanes))

    def fill(b, carry):
        tile = lax.rem(tile_s[0, b], tiles)
        kernel_plane = plane_s[0, b]
        spot = (cells[b, pl.ds(0, 1), :] + tile * side) * SHIFT + cells[b, pl.ds(1, 1), :]
        lookup = offsets[b] * (lanes // oversample) + kernel_plane
        records[b, pl.ds(0, 1), :] = encode(samples[b, pl.ds(0, 1), :], samples[b, pl.ds(1, 1), :], gain)
        records[b, pl.ds(1, 1), :] = spot
        records[b, pl.ds(2, 1), :] = lookup[0:1] * SHIFT + lookup[1:2]
        return carry

    lax.fori_loop(0, blocks, fill, 0, unroll=8)
    records[blocks, pl.ds(0, 3), :] = jnp.where(
        lax.broadcasted_iota(jnp.int32, (3, lanes), 0) == 1, tiles * side * SHIFT, 0
    )
    index_copy.wait()

    def outgoing(to):
        return send.at[to, pl.ds(0, out_rows)]

    def incoming(source):
        return got.at[source, pl.ds(0, out_rows)]

    def pack(to, carry):
        for j in range(capacity):
            s = to * capacity + j
            source = index_s[s // lanes, lax.rem(s, lanes)]
            send[to, pl.ds(j, 3, stride=capacity), :] = records[source, pl.ds(0, 3), :]
        send[to, pl.ds(3 * capacity, 1), :] = scale_row
        return carry

    lax.fori_loop(0, owners, pack, 0)
    own = pltpu.make_async_copy(outgoing(me), incoming(me), got_sem.at[me])
    own.start()
    pl.semaphore_wait(barrier, owners + 2)

    def each_partner(act):
        def visit(n, carry):
            act(n)
            return carry

        lax.fori_loop(1, owners, visit, 0)

    def outward(n):
        to = target(n)
        return pltpu.make_async_remote_copy(
            src_ref=outgoing(to), dst_ref=incoming(me), send_sem=send_sem.at[to], recv_sem=got_sem.at[me],
            device_id=(to, plane), device_id_type=MESH,
        )

    def arrival(n):
        source = origin(n)
        return pltpu.make_async_remote_copy(
            src_ref=outgoing(source), dst_ref=incoming(source), send_sem=send_sem.at[source],
            recv_sem=got_sem.at[source], device_id=(source, plane), device_id_type=MESH,
        )

    def homeward(n):
        to = origin(n)
        return pltpu.make_async_remote_copy(
            src_ref=solved.at[to, pl.ds(0, back_rows)], dst_ref=returned.at[me, pl.ds(0, back_rows)],
            send_sem=back_sem.at[to], recv_sem=home_sem.at[me], device_id=(to, plane), device_id_type=MESH,
        )

    each_partner(lambda n: outward(n).start())
    for load in loads[6:]:
        load.wait()
    for which in range(oversample):
        table_ref[:, pl.ds(which * (lanes // oversample), lanes // oversample)] = table_raw[which].astype(jnp.float32)
    model_t[...] = model[...].T
    total[...] = jnp.zeros_like(total)
    row1[...] = jnp.zeros_like(row1)
    weighted1[...] = jnp.zeros_like(weighted1)

    def add_grid(weighted, row):
        total[...] += lax.dot_general(
            row[...], weighted[...], (((1,), (1,)), ((), ())), preferred_element_type=jnp.float32
        )

    def chunk(n, turn, row, weighted, last_row, last_weighted):
        add_grid(last_weighted, last_row)
        work_chunk(got.at[origin(n)], model_t[...], table_ref[...], row, weighted, modelled.at[turn], capacity, side)

    def seal(n, turn):
        source = origin(n)
        real, imaginary = modelled[turn, pl.ds(0, capacity), :], modelled[turn, pl.ds(16, capacity), :]
        here = measure(jnp.maximum(jnp.abs(real), jnp.abs(imaginary)), MODEL_FRACTION)
        solved[source, pl.ds(0, capacity), :] = encode(
            real, imaginary, (LEVELS * MODEL_FRACTION) / here.astype(jnp.float32)
        )
        solved[source, pl.ds(capacity, 1), :] = jnp.broadcast_to(here, (1, lanes))

    late = chips_y - 1
    modelled[late] = jnp.zeros_like(modelled[late])

    def group(step, carry):
        first = chips_y * step
        for across in range(chips_y):
            arrival(first + across).wait_recv()
        seal(lax.rem(first + owners - 1, owners), late)
        for across in range(0, chips_y, 2):
            chunk(first + across, across, row0, weighted0, row1, weighted1)
            chunk(first + across + 1, across + 1, row1, weighted1, row0, weighted0)
        for across in range(late):
            seal(first + across, across)

        @pl.when(step > 0)
        def _():
            homeward(first - 1).start()
            homeward(first).start()

        for across in range(1, late):
            homeward(first + across).start()
        return carry

    lax.fori_loop(0, chips_z, group, 0)
    seal(owners - 1, late)
    homeward(owners - 1).start()
    add_grid(weighted1, row1)

    piece_rows = tiles * side // PIECES
    half = PIECES // 2

    def pass_on(which, piece, to, route):
        part = grids.at[which, pl.ds(piece * piece_rows, piece_rows)]
        return pltpu.make_async_remote_copy(
            src_ref=part, dst_ref=part, send_sem=grid_send.at[route, piece], recv_sem=grid_got.at[route, piece],
            device_id=(me, to), device_id_type=MESH,
        )

    started = []

    def launch(which, piece, to, route):
        copy = pass_on(which, piece, to, route)
        copy.start()
        started.append(copy)

    def came(which, piece, route):
        pass_on(which, piece, sibling, route).wait_recv()

    for piece in range(PIECES):
        spot = pl.ds(piece * piece_rows, piece_rows)
        grids[plane, spot, :] = total[spot, :].astype(jnp.bfloat16)
    for piece in range(PIECES):
        launch(plane, piece, ahead, 0)
        launch(plane, PIECES - 1 - piece, behind, 1)
    for piece in range(PIECES):
        launch(plane, piece, sibling, 4)
    for turn in range(PIECES):
        other = PIECES - 1 - turn
        came(behind, turn, 0)
        if turn < half:
            launch(behind, turn, ahead, 2)
        came(ahead, other, 1)
        if turn < half:
            launch(ahead, other, behind, 3)
        launch(behind, turn, sibling, 5)
        launch(ahead, other, sibling, 6)

    def collect(n, carry):
        source = target(n)
        pltpu.make_async_remote_copy(
            src_ref=solved.at[source, pl.ds(0, back_rows)], dst_ref=returned.at[source, pl.ds(0, back_rows)],
            send_sem=back_sem.at[source], recv_sem=home_sem.at[source], device_id=(source, plane), device_id_type=MESH,
        ).wait_recv()
        return carry

    lax.fori_loop(1, owners, collect, 0)
    returned[me, pl.ds(0, back_rows)] = solved[me, pl.ds(0, back_rows)]

    def unpack(b, carry):
        keeper = index_s[3, b]
        model_here = decode(
            returned[keeper, pl.ds(index_s[4, b], 1), :], returned[keeper, pl.ds(capacity, 1), :], MODEL_FRACTION
        )
        for part in range(2):
            residual_out[b, pl.ds(part, 1), :] = samples[b, pl.ds(part, 1), :] - model_here[part]
        return carry

    lax.fori_loop(0, blocks, unpack, 0, unroll=8)

    for turn in range(half):
        other = PIECES - 1 - turn
        came(opposite, turn, 2)
        launch(opposite, turn, sibling, 7)
        came(opposite, other, 3)
        launch(opposite, other, sibling, 7)

    def flip(which):
        return which + 1 - 2 * core

    share = coupling_v[pl.ds(plane, 1), :]
    number = lax.broadcasted_iota(jnp.int32, share.shape, 1)

    def term(which):
        part = jnp.sum(jnp.where(number == which, share, 0.0), axis=1, keepdims=True)
        return part * grids[which].astype(jnp.float32)

    coupled_out[...] = term(plane) + term(behind) + term(ahead) + term(opposite)
    for route, which in enumerate((sibling, flip(behind), flip(ahead), flip(opposite))):
        for piece in range(PIECES):
            came(which, piece, 4 + route)
    coupled_out[...] += term(sibling) + term(flip(behind)) + term(flip(ahead)) + term(flip(opposite))

    def settle(n):
        outward(n).wait_send()
        homeward(n).wait_send()

    each_partner(settle)
    for copy in started:
        copy.wait_send()


def body(visibilities, uv_cell, sub_pixel, w_plane, block_tile, model_grid, kernel_table, coupling):
    blocks = visibilities.shape[1]
    rows = visibilities.shape[3]
    owners = lax.axis_size("tile")
    capacity = 3 * blocks // owners
    tiles, side = model_grid.shape[1], model_grid.shape[2]
    oversample = kernel_table.shape[1]
    planes = lax.axis_size("freq")
    chips_x, chips_y = planes // 2, 4
    vmem = pl.BlockSpec(memory_space=pltpu.VMEM)
    hbm = pl.BlockSpec(memory_space=pltpu.HBM)
    copies = pltpu.SemaphoreType.DMA
    taps = (tiles * side, capacity * rows)
    operands = (
        block_tile,
        w_plane,
        coupling,
        visibilities[0],
        uv_cell[0],
        sub_pixel[0],
        model_grid.reshape(tiles * side, 2 * side),
        kernel_table.transpose(1, 2, 0),
    )
    residuals, coupled = pl.pallas_call(
        functools.partial(kernel, (owners, capacity, tiles, side, oversample, chips_y, chips_x)),
        out_shape=(
            jax.ShapeDtypeStruct((blocks, 2, rows), jnp.float32),
            jax.ShapeDtypeStruct((tiles * side, 2 * side), jnp.float32),
        ),
        in_specs=[hbm] * len(operands),
        out_specs=[vmem] * 2,
        scratch_shapes=[
            pltpu.SMEM((1, blocks), jnp.int32),
            pltpu.SMEM((1, blocks), jnp.int32),
            pltpu.VMEM((1, blocks), jnp.int32),
            pltpu.VMEM((planes, planes), jnp.float32),
            pltpu.VMEM((blocks, 2, rows), jnp.float32),
            pltpu.VMEM((blocks, 2, rows), jnp.int32),
            pltpu.VMEM((blocks, 2, rows), jnp.int32),
            pltpu.VMEM((tiles * side, 2 * side), jnp.bfloat16),
            pltpu.VMEM(operands[-1].shape, jnp.bfloat16),
            pltpu.VMEM((8, rows), jnp.float32),
            pltpu.VMEM((blocks + 1, 4, rows), jnp.int32),
            pltpu.VMEM((8, rows), jnp.int32),
            pltpu.SMEM((8, rows), jnp.int32),
            pltpu.VMEM((chips_y, 32, rows), jnp.float32),
            pltpu.VMEM((2 * side, tiles * side), jnp.bfloat16),
            pltpu.VMEM((owners, 40, rows), jnp.int32),
            pltpu.VMEM((owners, 40, rows), jnp.int32),
            pltpu.VMEM((owners, 16, rows), jnp.int32),
            pltpu.VMEM((owners, 16, rows), jnp.int32),
            pltpu.VMEM(taps, jnp.bfloat16),
            pltpu.VMEM(taps, jnp.bfloat16),
            pltpu.VMEM(taps, jnp.bfloat16),
            pltpu.VMEM(taps, jnp.bfloat16),
            pltpu.VMEM((tiles * side, 2 * side), jnp.float32),
            pltpu.VMEM((planes, tiles * side, 2 * side), jnp.bfloat16),
            copies((len(operands) + 1,)),
            copies,
            copies((owners,)),
            copies((owners,)),
            copies((owners,)),
            copies((owners,)),
            copies((8, PIECES)),
            copies((8, PIECES)),
        ],
        compiler_params=pltpu.CompilerParams(collective_id=0, has_side_effects=True, vmem_limit_bytes=40 << 20),
    )(*(pltpu.with_memory_space_constraint(operand, pltpu.HBM) for operand in operands))
    return residuals[None], coupled.reshape(1, tiles, side, 2 * side)


def solution(mesh):
    return jax.shard_map(
        body,
        mesh=mesh,
        in_specs=(
            P("freq", "tile", None, None),
            P("freq", "tile", None, None),
            P("freq", "tile", None, None),
            P("freq", "tile"),
            P("freq", "tile"),
            P("freq", "tile", None, None),
            P(),
            P(),
        ),
        out_specs=(P("freq", "tile", None, None), P("freq", "tile", None, None)),
        check_vma=False,
    )
```
